128 devices in a mesh: section: 8 (over x, core), tp: 16 (over z, y).
Axes of the slice: x: 4, y: 4, z: 4, core: 2. Of those that a mesh axis runs over, the one named last changes fastest.
Arguments:
- layer_inputs: bfloat16 [16, 512, 4096], P('section', None, 'tp'), may hold values from -6 to 6
- weights: bfloat16 [16, 4096, 4096], P('section', 'tp'), may hold values from -0.046875 to 0.046875
- input_basis: bfloat16 [16, 4096, 64], P('section', 'tp'), may hold values from -0.09375 to 0.09375
- output_basis: bfloat16 [16, 4096, 32], P('section', 'tp'), may hold values from -0.09375 to 0.09375
- queries: bfloat16 [16, 512, 2048], P('section', 'tp'), may hold values from -0.00390625 to 0.00390625
- top_cotangent: bfloat16 [512, 4096], replicated, may hold values from -6 to 6
- sequence_example: int32 [4], replicated, may hold values from 0 to 1
Outputs:
- scores: float32 [2, 512], P(None, 'tp')
The draws below stay inside these ranges and needn't reach their ends.
All inputs are finite; a program needn't handle non-finite values.
Results may differ from the reference program's by a relative error of at most 0.0094.
Values may be sent and summed in bfloat16 or wider, within the bound.
No kernel may reach another device: no remote copies, remote signals or barrier semaphores. Data moves between devices by JAX's collectives and lax.ppermute only.
A program may use at most 64 MiB of HBM per device.

```python
import jax
import jax.numpy as jnp
from jax import lax

D = 4096
RIN = 64
ROUT = 32
NQ = 512
SEQLEN = 128
LAYERS = 16
KDIM = 2048
SEQS = 4
TOKENS = 512
EXAMPLES = 2


def set_ends(values, stream_key, low, high):
    shape = values.shape
    spot = [jax.random.randint(jax.random.fold_in(stream_key, axis), (), 0, shape[axis]) for axis in range(len(shape))]
    values = values.at[tuple(spot)].set(low)
    longest = shape.index(max(shape))
    spot[longest] = (spot[longest] + 1) % shape[longest]
    return values.at[tuple(spot)].set(high)


def block_scale(own_key, extent, split, least, top_value):
    def one(axis_at, parts):
        steps = jax.random.uniform(jax.random.fold_in(jax.random.fold_in(own_key, 6), axis_at), (parts,), jnp.float32, least / len(split), top_value / len(split))
        return jnp.repeat(jnp.exp(steps), extent[axis_at] // parts).reshape((-1,) + (1,) * (len(extent) - axis_at - 1))

    factor_of = one(*split[0])
    for cut in split[1:]:
        factor_of = factor_of * one(*cut)
    return factor_of


def scatter_about(key, shape, deviation, most, pieces=(), kind=jnp.bfloat16):
    drawn = jax.random.normal(key, shape, jnp.float32) * deviation
    if len(pieces) > 0:
        drawn = block_scale(key, shape, pieces, -0.22, 0.18) * drawn
    return jnp.clip(drawn, min=-most, max=most).astype(kind)


def setup_inputs(seed: int = 0) -> dict:
    streams_of = jax.random.split(jax.random.key(seed), 8)
    layer_inputs = scatter_about(streams_of[0], (LAYERS, TOKENS, D), 1.0, 6.0, ((0, 8), (2, 16)))
    weights = scatter_about(streams_of[1], (LAYERS, D, D), (4 * D) ** -0.5, 0.046875, ((0, 8), (1, 16)))
    input_basis = scatter_about(streams_of[2], (LAYERS, D, RIN), D ** -0.5, 0.09375, ((0, 8), (1, 16)))
    output_basis = scatter_about(streams_of[3], (LAYERS, D, ROUT), D ** -0.5, 0.09375, ((0, 8), (1, 16)))
    queries = scatter_about(streams_of[4], (LAYERS, NQ, KDIM), (KDIM * 1024) ** -0.5, 0.00390625, ((0, 8), (1, 16)))
    top_cotangent = scatter_about(streams_of[5], (TOKENS, D), 1.0, 6.0)
    sequence_example = set_ends(jax.random.randint(streams_of[6], (SEQS,), 0, EXAMPLES), jax.random.fold_in(streams_of[6], 1), 0, EXAMPLES - 1).astype(jnp.int32)
    return dict(layer_inputs=layer_inputs, weights=weights, input_basis=input_basis, output_basis=output_basis, queries=queries, top_cotangent=top_cotangent, sequence_example=sequence_example)


def reference(layer_inputs, weights, input_basis, output_basis, queries, top_cotangent, sequence_example):
    token_examples = jnp.repeat(sequence_example, SEQLEN)
    selector = (jnp.arange(EXAMPLES, dtype=jnp.int32)[:, None] == token_examples[None, :]).astype(jnp.float32)

    def layer_step(cotangent, inputs):
        hidden, matrix, basis_in, basis_out, stored_queries = inputs
        floats = hidden.astype(jnp.float32)
        logistic = jax.nn.sigmoid(floats)
        activated = (floats * logistic).astype(jnp.bfloat16)
        slope = logistic * (1.0 + floats * (1.0 - logistic))
        in_feats = jnp.dot(activated, basis_in, preferred_element_type=jnp.float32)
        out_feats = jnp.dot(cotangent, basis_out, preferred_element_type=jnp.float32)
        joined = (out_feats[:, :, None] * in_feats[:, None, :]).reshape(out_feats.shape[0], -1)
        grads = jnp.dot(selector, joined, precision=lax.Precision.HIGHEST)
        layer_scores = jnp.dot(grads, stored_queries.astype(jnp.float32).T, precision=lax.Precision.HIGHEST)
        branch = jnp.dot(cotangent, matrix.T, preferred_element_type=jnp.float32)
        updated = (cotangent.astype(jnp.float32) + slope * branch).astype(jnp.bfloat16)
        return updated, layer_scores

    final, stacked = lax.scan(layer_step, top_cotangent, (layer_inputs, weights, input_basis, output_basis, queries), reverse=True)
    return jnp.sum(stacked, axis=0)
```

```python
import functools

import jax
import jax.numpy as jnp
from jax import lax
from jax.experimental import pallas as pl
from jax.experimental.pallas import tpu as pltpu
from jax.sharding import Mesh, PartitionSpec as P

AXES = ("x", "c", "z", "y")
SIZES = {"x": 4, "c": 2, "z": 4, "y": 4}
ALL = (0, 1, 2, 3)
SEQ = 128
RIN = 64
ROUT = 32
LANES = 128
EXAMPLES = 2
F32 = jnp.float32
BF16 = jnp.bfloat16
HIGH = lax.Precision.HIGHEST
NT = (((1,), (1,)), ((), ()))


def linear(x, c, z, y):
    return ((x * 2 + c) * 4 + z) * 4 + y


def shift(value, axis, by, planes=ALL):
    at = AXES.index(axis)
    pairs = []
    for x in planes:
        for c in range(2):
            for z in range(4):
                for y in range(4):
                    here = [x, c, z, y]
                    there = list(here)
                    there[at] = (here[at] + by) % SIZES[axis]
                    pairs.append((linear(*there), linear(*here)))
    return lax.ppermute(value, AXES, pairs)


def down(value, plane):
    pairs = []
    for c in range(2):
        for z in range(4):
            for y in range(4):
                pairs.append((linear(plane, c, z, y), linear(plane - 1, c, z, y)))
    return lax.ppermute(value, AXES, pairs)


def ring(pieces, place):
    stacked = jnp.stack(list(pieces) + list(pieces), 0)
    return lax.dynamic_slice_in_dim(stacked, (4 - place) % 4, 4, 0)


def arrange_body(place, source, own, other):
    core = place[0]
    y = place[1]
    for m in range(4):
        for block in range(4):
            start = block * 1024 + ((y + m) % 4) * 256
            to = pl.ds((m * 4 + block) * LANES, LANES)
            mine = pl.multiple_of(start + core * LANES, LANES)
            theirs = pl.multiple_of(start + (1 - core) * LANES, LANES)
            own[0, :, to] = source[0, :, pl.ds(mine, LANES)]
            other[0, :, to] = source[0, :, pl.ds(theirs, LANES)]


def arrange(place, source, swap_rows):
    groups, rows, width = source.shape
    steps = rows // LANES
    if swap_rows:
        own_map = lambda g, r, place: (g, (r + place[0]) % 2, 0)
        other_map = lambda g, r, place: (g, (r + 1 - place[0]) % 2, 0)
    else:
        own_map = other_map = lambda g, r, place: (g, r, 0)
    half = (groups, rows, width // 2)
    return pl.pallas_call(
        arrange_body,
        grid_spec=pltpu.PrefetchScalarGridSpec(
            num_scalar_prefetch=1,
            grid=(groups, steps),
            in_specs=[pl.BlockSpec((1, LANES, width), lambda g, r, place: (g, r, 0))],
            out_specs=[
                pl.BlockSpec((1, LANES, width // 2), own_map),
                pl.BlockSpec((1, LANES, width // 2), other_map),
            ],
        ),
        out_shape=[jax.ShapeDtypeStruct(half, source.dtype)] * 2,
    )(place, source)


def branch_body(place, c0, c1, c2, c3, w0, w1, w2, w3, keep, send, wide, sems):
    z = place[2]
    copies = []
    for k, ref in enumerate((w0, w1, w2, w3)):
        copy = pltpu.make_async_copy(ref, wide.at[k], sems.at[k])
        copy.start()
        copies.append(copy)
    joined = jnp.concatenate([ref[i] for ref in (c0, c1, c2, c3) for i in range(4)], 1)
    for k in range(4):
        copies[k].wait()
        product = lax.dot_general(joined, wide[k], NT, preferred_element_type=F32)
        at = (z + k) % 4
        keep[at] = product[:, :LANES]
        send[at] = product[:, LANES:]


def branch(place, parts, blocks):
    vmem = pl.BlockSpec(memory_space=pltpu.VMEM)
    shape = jax.ShapeDtypeStruct((4, SEQ, LANES), F32)
    rows, depth = blocks[0].shape
    return pl.pallas_call(
        branch_body,
        in_specs=[pl.BlockSpec(memory_space=pltpu.SMEM)]
        + [vmem] * 4
        + [pl.BlockSpec(memory_space=pl.ANY)] * 4,
        out_specs=[vmem, vmem],
        out_shape=[shape, shape],
        scratch_shapes=[
            pltpu.VMEM((4, rows, depth), BF16),
            pltpu.SemaphoreType.DMA((4,)),
        ],
        cost_estimate=pl.CostEstimate(
            flops=2 * SEQ * 4 * rows * depth,
            bytes_accessed=4 * rows * depth * 2,
            transcendentals=0,
        ),
    )(place, *parts, *blocks)


def halves(value, core):
    low, high = value[..., :LANES], value[..., LANES:]
    first = core == 0
    return jnp.where(first, low, high), jnp.where(first, high, low)


def by_layer(own, received, core):
    first = core == 0
    return [jnp.where(first, own[0], received[0]), jnp.where(first, own[1], received[1])] + [
        jnp.where(first, received[0], own[0]),
        jnp.where(first, received[1], own[1]),
    ]


def slope_of(hidden):
    floats = hidden.astype(F32)
    logistic = jax.nn.sigmoid(floats)
    return logistic * (1.0 + floats * (1.0 - logistic))


def activate(hidden):
    floats = hidden.astype(F32)
    return (floats * jax.nn.sigmoid(floats)).astype(BF16)


def shards(
    layer_inputs, weights, input_basis, output_basis, queries, top_cotangent, sequence_example
):
    x = lax.axis_index("x")
    core = lax.axis_index("c")
    z = lax.axis_index("z")
    y = lax.axis_index("y")
    place = jnp.stack([core, y, z]).astype(jnp.int32)

    own_w, other_w = arrange(place, weights, True)
    swapped = [shift(other_w[i], "c", 1) for i in range(2)]
    own_half = by_layer(own_w, swapped, core)

    gathered = [None] * 4

    def fetch(j, planes=ALL):
        return [shift(own_half[j], "z", k, planes) for k in (1, 2, 3)]

    keep_h, send_h = halves(layer_inputs, core)
    basis = jnp.concatenate([input_basis, output_basis], 2)
    basis = jnp.swapaxes(basis, 1, 2)
    keep_b, send_b = halves(basis, core)
    got = shift(jnp.concatenate([send_h, send_b], 1), "c", 1)
    small = jnp.stack(by_layer(jnp.concatenate([keep_h, keep_b], 1), got, core), 0)
    tokens = layer_inputs.shape[1]
    hidden_natural = small[:, :tokens]
    basis_natural = small[:, tokens:]

    def for_row(k):
        row = (z + 4 - k) % 4
        piece = lax.dynamic_slice_in_dim(hidden_natural, row * SEQ, SEQ, 1)
        return jnp.concatenate([piece, basis_natural], 1)

    small_parts = [for_row(0)] + [shift(for_row(k), "z", k) for k in (1, 2, 3)]
    gathered[2] = fetch(2)
    here = ring(small_parts, z)
    hidden = here[:, :, :SEQ]
    in_basis = here[:, :, SEQ : SEQ + RIN]
    out_basis = here[:, :, SEQ + RIN :]

    in_part = jnp.einsum("zjtc,zjrc->jtr", activate(hidden), in_basis, preferred_element_type=F32)
    in_half = in_part + shift(in_part, "c", 1)
    in_feats = in_half + shift(in_half, "y", 1) + shift(in_half, "y", 2) + shift(in_half, "y", 3)

    top_own, _ = arrange(place, top_cotangent[None], False)
    product = lax.dot_general(top_own[0], own_half[3], NT, preferred_element_type=F32)
    total = product[:, :LANES] + shift(product[:, LANES:], "c", 1, (3,))
    column = (z * 4 + y) * 256 + core * LANES
    top_natural = lax.dynamic_slice(top_cotangent, (0, column), (tokens, LANES))
    below_top = (top_natural.astype(F32) + slope_of(hidden_natural[3]) * total).astype(BF16)

    def row_piece(value, k):
        return lax.dynamic_slice_in_dim(value, ((z + 4 - k) % 4) * SEQ, SEQ, 0)

    first = [row_piece(below_top, 0)]
    first += [shift(row_piece(below_top, k), "z", k, (3,)) for k in (1, 2, 3)]
    state = ring(first, z)
    top_here = jnp.stack(
        [
            lax.dynamic_slice(
                top_cotangent, (z * SEQ, b * 1024 + y * 256 + core * LANES), (SEQ, LANES)
            )
            for b in range(4)
        ],
        0,
    )

    order = {2: ((3, (0, 1, 2)), (1, ALL)), 1: ((0, ALL),)}
    out_part = None
    for plane in (3, 2, 1, 0):
        seen = [None] * 4
        for j in (3, 2, 1, 0):
            if plane == 3 and j == 3:
                seen[j] = top_here
                continue
            seen[j] = state
            blocks = [own_half[j]] + gathered[j]
            if plane == 3 and j in order:
                held = [own_half[n] for n, _ in order[j]]
                blocks, held = lax.optimization_barrier((blocks, held))
                for (n, planes), value in zip(order[j], held):
                    gathered[n] = [shift(value, "z", k, planes) for k in (1, 2, 3)]
            parts = [state] + [shift(state, "y", m, (plane,)) for m in (1, 2, 3)]
            keep, send = branch(place, parts, blocks)
            total = keep + shift(send, "c", 1, (plane,))
            state = (state.astype(F32) + slope_of(hidden[:, j]) * total).astype(BF16)
        part = jnp.einsum(
            "jztc,zjrc->jtr", jnp.stack(seen, 0), out_basis, preferred_element_type=F32
        )
        out_part = part if out_part is None else jnp.where(x == plane, part, out_part)
        if plane > 0:
            state = down(state, plane)

    out_half = out_part + shift(out_part, "c", 1)
    out_feats = (
        out_half + shift(out_half, "y", 1) + shift(out_half, "y", 2) + shift(out_half, "y", 3)
    )
    grads = jnp.einsum("jto,jti->joi", out_feats, in_feats, precision=HIGH)
    grads = lax.dynamic_slice_in_dim(grads, 2 * core, 2, 0).reshape(2, ROUT * RIN)
    rows = jnp.stack([grads] + [shift(grads, "z", k) for k in (1, 2, 3)], 1)
    scores = jnp.einsum("lsk,lqk->sq", rows, queries.astype(F32), precision=HIGH)
    examples = jnp.stack([sequence_example[(z + k) % 4] for k in range(4)])
    select = jnp.arange(EXAMPLES, dtype=jnp.int32)[:, None, None] == examples[None, :, None]
    scores = jnp.sum(jnp.where(select, scores[None], 0.0), 1)
    scores = scores + shift(scores, "c", 1)
    return scores + shift(scores, "x", 1) + shift(scores, "x", 2) + shift(scores, "x", 3)


def solution(mesh):
    fine = Mesh(mesh.devices.reshape(4, 2, 4, 4), AXES)
    section = ("x", "c")
    tp = ("z", "y")
    placed = (
        P(section, None, tp),
        P(section, tp, None),
        P(section, tp, None),
        P(section, tp, None),
        P(section, tp, None),
        P(),
        P(),
    )
    return jax.shard_map(
        shards, mesh=fine, in_specs=placed, out_specs=P(None, tp), check_vma=False
    )
```

```python
import jax
import jax.numpy as jnp
from jax import lax
from jax.experimental import pallas as pl
from jax.experimental.pallas import tpu as pltpu
from jax.sharding import Mesh, PartitionSpec as P

AXES = ("x", "c", "z", "y")
SIZES = {"x": 4, "c": 2, "z": 4, "y": 4}
SEQ = 128
RIN = 64
ROUT = 32
LANES = 128
EXAMPLES = 2
F32 = jnp.float32
BF16 = jnp.bfloat16
HIGH = lax.Precision.HIGHEST
NT = (((1,), (1,)), ((), ()))


def shift(value, axis, by):
    size = SIZES[axis]
    return lax.ppermute(value, axis, [((i + by) % size, i) for i in range(size)])


def others(value, axis):
    return [shift(value, axis, by) for by in range(1, SIZES[axis])]


def arrange_body(place, source, own_a, own_b, other_a, other_b):
    core = place[0]
    y = place[1]
    for g, own, other in ((0, own_a, other_a), (1, own_b, other_b)):
        layer = (g + place[3]) % 2
        for m in range(4):
            for block in range(4):
                start = block * 1024 + ((y + m) % 4) * 256
                to = pl.ds((m * 4 + block) * LANES, LANES)
                mine = pl.multiple_of(start + core * LANES, LANES)
                theirs = pl.multiple_of(start + (1 - core) * LANES, LANES)
                own[:, to] = source[layer, :, pl.ds(mine, LANES)]
                other[:, to] = source[layer, :, pl.ds(theirs, LANES)]


def arrange(place, source):
    groups, rows, width = source.shape
    step = 64
    per = LANES // step
    own_map = lambda r, place: ((r // per + place[0]) % 2 * per + r % per, 0)
    other_map = lambda r, place: ((r // per + 1 - place[0]) % 2 * per + r % per, 0)
    half = (step, width // 2)
    shape = jax.ShapeDtypeStruct((rows, width // 2), source.dtype)
    return pl.pallas_call(
        arrange_body,
        grid_spec=pltpu.PrefetchScalarGridSpec(
            num_scalar_prefetch=1,
            grid=(rows // step,),
            in_specs=[pl.BlockSpec((groups, step, width), lambda r, place: (0, r, 0))],
            out_specs=[pl.BlockSpec(half, own_map)] * 2 + [pl.BlockSpec(half, other_map)] * 2,
        ),
        out_shape=[shape] * 4,
        compiler_params=pltpu.CompilerParams(vmem_limit_bytes=8 * 2**20),
    )(place, source)


def branch_body(place, c0, c1, c2, c3, w0, w1, low, high, w3, keep, send, joined):
    z = place[2]
    for m, ref in enumerate((c0, c1, c2, c3)):
        for block in range(4):
            joined[pl.ds((m * 4 + block) * LANES, LANES)] = ref[(block + 4 - z) % 4]
    for k, ref in ((0, w0), (1, w1), (3, w3)):
        part = jnp.dot(ref[...], joined[...], preferred_element_type=F32)
        keep[k] = part[:LANES]
        send[k] = part[LANES:]
    keep[2] = jnp.dot(low[...], joined[...], preferred_element_type=F32)
    send[2] = jnp.dot(high[...], joined[...], preferred_element_type=F32)


def branch(place, parts, blocks):
    vmem = pl.BlockSpec(memory_space=pltpu.VMEM)
    shape = jax.ShapeDtypeStruct((4, LANES, SEQ), F32)
    rows, depth = blocks[0].shape
    return pl.pallas_call(
        branch_body,
        in_specs=[pl.BlockSpec(memory_space=pltpu.SMEM)] + [vmem] * 9,
        out_specs=[vmem, vmem],
        out_shape=[shape, shape],
        scratch_shapes=[pltpu.VMEM((depth, SEQ), BF16)],
        compiler_params=pltpu.CompilerParams(vmem_limit_bytes=8 * 2**20),
        cost_estimate=pl.CostEstimate(
            flops=2 * SEQ * 4 * rows * depth,
            bytes_accessed=4 * rows * depth * 2,
            transcendentals=0,
        ),
    )(place, *parts, *blocks)


def slope_of(hidden):
    floats = hidden.astype(F32)
    logistic = jax.nn.sigmoid(floats)
    return logistic * (1.0 + floats * (1.0 - logistic))


def activate(hidden):
    floats = hidden.astype(F32)
    return (floats * jax.nn.sigmoid(floats)).astype(BF16)


def first_fetch(block):
    return [shift(block, "z", 1), shift(block, "z", 3)]


def second_fetch(near):
    return [shift(near[0][:LANES], "z", 1), shift(near[1][LANES:], "z", 3)]


def shards(
    layer_inputs, weights, input_basis, output_basis, queries, top_cotangent, sequence_example
):
    x = lax.axis_index("x")
    core = lax.axis_index("c")
    z = lax.axis_index("z")
    y = lax.axis_index("y")
    is_top = x == 3
    tokens = layer_inputs.shape[1]
    width = layer_inputs.shape[2]
    flip = jnp.where(is_top & (core == 1), 0, 1)
    place = jnp.stack([core, y, z, flip]).astype(jnp.int32)

    basis = jnp.concatenate([input_basis, output_basis], 2)
    basis = jnp.pad(basis, ((0, 0), (0, 0), (0, LANES - RIN - ROUT)))
    mixed = [
        jnp.concatenate(
            [layer_inputs[:, :, h * LANES : (h + 1) * LANES], basis[:, h * LANES : (h + 1) * LANES]],
            1,
        )
        for h in range(2)
    ]
    upper = core == 1
    mine = jnp.where(upper, mixed[1], mixed[0])
    got = shift(jnp.where(upper, mixed[0], mixed[1]), "c", 1)
    small = jnp.where(upper, jnp.concatenate([got, mine], 0), jnp.concatenate([mine, got], 0))

    def for_row(k):
        piece = lax.dynamic_slice_in_dim(small, (z + 4 - k) % 4 * SEQ, SEQ, 1)
        return jnp.concatenate([piece, small[:, tokens:]], 1)

    outgoing = [for_row(k) for k in range(4)]
    here = [outgoing[0]] + [shift(outgoing[k], "z", k) for k in (1, 2, 3)]

    cotangent, _ = lax.optimization_barrier((top_cotangent, outgoing))
    product = lax.dot_general(cotangent, weights[1], NT, preferred_element_type=F32)
    top_own = lax.dynamic_slice(top_cotangent, (0, (z * 4 + y) * width), (tokens, width))
    below_top = (top_own.astype(F32) + slope_of(layer_inputs[1]) * product).astype(BF16)
    given = shift(below_top[:, :LANES], "c", 1)
    below_half = jnp.where(upper, below_top[:, LANES:], given)

    def row_piece(k):
        return lax.dynamic_slice_in_dim(below_half, (z + 4 - k) % 4 * SEQ, SEQ, 0)

    first = jnp.stack([row_piece(0)] + [shift(row_piece(k), "z", k) for k in (1, 2, 3)], 0)

    held, _, here = lax.optimization_barrier((weights, below_top, here))
    own_a, own_b, other_a, other_b = arrange(place, held)
    own_w = (own_a, own_b)
    swapped = [shift(other_a, "c", 1), shift(other_b, "c", 1)]
    slots = [jnp.where(upper, own_w[0], swapped[0])]
    slots[0], first, here = lax.optimization_barrier((slots[0], first, here))
    state = jnp.swapaxes(first, 1, 2)
    near = [first_fetch(slots[0])] + [None] * 3
    far = [None] * 4
    a0, a1, b0, b1 = lax.optimization_barrier((own_w[0], own_w[1], swapped[0], swapped[1]))
    slots.append(jnp.where(is_top, jnp.where(upper, b0, a0), jnp.where(upper, a1, b1)))
    slots.append(
        jnp.where(is_top, jnp.where(upper, b1, a1), jnp.where(upper, b0, a0))
    )
    slots.append(jnp.where(is_top, jnp.where(upper, a1, b1), jnp.where(upper, b1, a1)))

    here = jnp.stack(here, 0)
    hidden = jnp.swapaxes(here[:, :, :SEQ], 2, 3)
    basis = jnp.transpose(here[:, :, SEQ:], (1, 3, 0, 2)).reshape(4, LANES, 4 * LANES)
    in_basis = basis[:, :RIN]
    out_basis = basis[:, RIN : RIN + ROUT]
    active = activate(hidden)
    in_part = jnp.stack(
        [
            jnp.dot(in_basis[j], active[:, j].reshape(-1, SEQ), preferred_element_type=F32)
            for j in range(4)
        ],
        0,
    )
    in_half = in_part + shift(in_part, "c", 1)
    in_feats = in_half + sum(others(in_half, "y"))
    slopes, out_basis = lax.optimization_barrier(
        ([slope_of(hidden[:, j]) for j in range(4)], [out_basis[j] for j in range(4)])
    )

    top_here = jnp.stack(
        [
            lax.dynamic_slice(
                top_cotangent,
                (z * SEQ, (z + k) % 4 * 1024 + y * 256 + core * LANES),
                (SEQ, LANES),
            )
            for k in range(4)
        ],
        0,
    )
    top_here = jnp.swapaxes(top_here, 1, 2)

    def advance(slot, state):
        near[slot], _ = lax.optimization_barrier((near[slot], state))
        far[slot] = second_fetch(near[slot])
        far[slot], slots[slot + 1] = lax.optimization_barrier((far[slot], slots[slot + 1]))
        near[slot + 1] = first_fetch(slots[slot + 1])

    out_part = [None] * 4
    for plane in (3, 2, 1, 0):
        for j in (3, 2, 1, 0):
            seen = top_here if plane == 3 and j == 3 else state
            part = jnp.dot(out_basis[j], seen.reshape(-1, SEQ), preferred_element_type=F32)
            out_part[j] = part if plane == 3 else jnp.where(x == plane, part, out_part[j])
            if plane == 3 and j == 3:
                continue
            slot = 2 - j if plane == 3 else 3 - j
            if plane == 3:
                advance(slot, state)
            elif far[slot] is None:
                far[slot] = second_fetch(near[slot])
            blocks = [slots[slot], near[slot][0], far[slot][0], far[slot][1], near[slot][1]]
            keep, send = branch(place, [state] + others(state, "y"), blocks)
            total = keep + shift(send, "c", 1)
            state = (state.astype(F32) + slopes[j] * total).astype(BF16)
        if plane > 0:
            state = shift(state, "x", 1)

    out_part = jnp.stack(out_part, 0)
    out_half = out_part + shift(out_part, "c", 1)
    out_feats = out_half + sum(others(out_half, "y"))
    grads = jnp.einsum("jot,jit->joi", out_feats, in_feats, precision=HIGH)
    grads = lax.dynamic_slice_in_dim(grads, 2 * core, 2, 0).reshape(2, ROUT * RIN)
    rows = jnp.stack([grads] + others(grads, "z"), 1)
    scores = jnp.einsum("lsk,lqk->sq", rows, queries.astype(F32), precision=HIGH)
    examples = jnp.stack([sequence_example[(z + k) % 4] for k in range(4)])
    select = jnp.arange(EXAMPLES, dtype=jnp.int32)[:, None, None] == examples[None, :, None]
    scores = jnp.sum(jnp.where(select, scores[None], 0.0), 1)
    scores = scores + shift(scores, "c", 1)
    return scores + sum(others(scores, "x"))


def solution(mesh):
    fine = Mesh(mesh.devices.reshape(4, 2, 4, 4), AXES)
    section = ("x", "c")
    tp = ("z", "y")
    placed = (
        P(section, None, tp),
        P(section, tp, None),
        P(section, tp, None),
        P(section, tp, None),
        P(section, tp, None),
        P(),
        P(),
    )
    return jax.shard_map(
        shards, mesh=fine, in_specs=placed, out_specs=P(None, tp), check_vma=False
    )
```

```python
import jax
import jax.numpy as jnp
from jax import lax
from jax.experimental import pallas as pl
from jax.experimental.pallas import tpu as pltpu
from jax.sharding import Mesh, PartitionSpec as P

AXES = ("x", "c", "z", "y")
SIZES = {"x": 4, "c": 2, "z": 4, "y": 4}
SEQ = 128
RIN = 64
ROUT = 32
PART = 128 + RIN + ROUT
LANES = 128
EXAMPLES = 2
F32 = jnp.float32
BF16 = jnp.bfloat16
HIGH = lax.Precision.HIGHEST
NT = (((1,), (1,)), ((), ()))


def shift(value, axis, by):
    size = SIZES[axis]
    return lax.ppermute(value, axis, [((i + by) % size, i) for i in range(size)])


def others(value, axis):
    return [shift(value, axis, by) for by in range(1, SIZES[axis])]


def arrange_body(place, source, own_a, own_b, other_a, other_b):
    core = place[0]
    y = place[1]
    for g, own, other in ((0, own_a, other_a), (1, own_b, other_b)):
        layer = (g + place[3]) % 2
        for m in range(4):
            for block in range(4):
                start = block * 1024 + ((y + m) % 4) * 256
                to = pl.ds((m * 4 + block) * LANES, LANES)
                mine = pl.multiple_of(start + core * LANES, LANES)
                theirs = pl.multiple_of(start + (1 - core) * LANES, LANES)
                own[:, to] = source[layer, :, pl.ds(mine, LANES)]
                other[:, to] = source[layer, :, pl.ds(theirs, LANES)]


def arrange(place, source):
    groups, rows, width = source.shape
    step = 64
    per = LANES // step
    own_map = lambda r, place: ((r // per + place[0]) % 2 * per + r % per, 0)
    other_map = lambda r, place: ((r // per + 1 - place[0]) % 2 * per + r % per, 0)
    half = (step, width // 2)
    shape = jax.ShapeDtypeStruct((rows, width // 2), source.dtype)
    return pl.pallas_call(
        arrange_body,
        grid_spec=pltpu.PrefetchScalarGridSpec(
            num_scalar_prefetch=1,
            grid=(rows // step,),
            in_specs=[pl.BlockSpec((groups, step, width), lambda r, place: (0, r, 0))],
            out_specs=[pl.BlockSpec(half, own_map)] * 2 + [pl.BlockSpec(half, other_map)] * 2,
        ),
        out_shape=[shape] * 4,
        compiler_params=pltpu.CompilerParams(vmem_limit_bytes=8 * 2**20),
    )(place, source)


SMALL_VMEM = pltpu.CompilerParams(vmem_limit_bytes=6 * 2**20)
VMEM = pl.BlockSpec(memory_space=pltpu.VMEM)
SMEM = pl.BlockSpec(memory_space=pltpu.SMEM)


def split_body(place, inputs, in_basis, out_basis, mine, send):
    core = place[0]
    tokens = inputs.shape[1]
    for target, half in ((mine, core), (send, 1 - core)):
        lanes = pl.ds(pl.multiple_of(half * LANES, LANES), LANES)
        for i in range(2):
            target[i, pl.ds(0, tokens)] = inputs[i, :, lanes]
            target[i, pl.ds(tokens, RIN)] = in_basis[i, :, lanes]
            target[i, pl.ds(tokens + RIN, ROUT)] = out_basis[i, :, lanes]


def split(place, inputs, in_basis, out_basis):
    shape = jax.ShapeDtypeStruct((2, inputs.shape[1] + RIN + ROUT, LANES), BF16)
    return pl.pallas_call(
        split_body,
        in_specs=[SMEM] + [VMEM] * 3,
        out_specs=[VMEM] * 2,
        out_shape=[shape] * 2,
        compiler_params=SMALL_VMEM,
    )(place, inputs, in_basis, out_basis)


def rows_body(place, mine, got, full, given, o0, o1, o2, o3):
    core = place[0]
    z = place[2]
    tokens = mine.shape[1] - RIN - ROUT
    for source, owner in ((mine, core), (got, 1 - core)):
        for i in range(2):
            layer = owner * 2 + i
            start = pl.multiple_of(layer * PART, 16)
            for k, target in enumerate((o0, o1, o2, o3)):
                at = pl.multiple_of((z + 4 - k) % 4 * SEQ, SEQ)
                target[pl.ds(start, LANES)] = source[i, pl.ds(at, SEQ)].T
                target[pl.ds(start + LANES, RIN + ROUT)] = source[i, pl.ds(tokens, RIN + ROUT)]
    for k, target in enumerate((o0, o1, o2, o3)):
        at = pl.ds(pl.multiple_of((z + 4 - k) % 4 * SEQ, SEQ), SEQ)
        own = full[at, LANES:].astype(F32)
        other = given[at].astype(F32)
        target[pl.ds(4 * PART, LANES)] = jnp.where(core == 1, own, other).T.astype(BF16)


def rows_of(place, mine, got, full, given):
    shape = jax.ShapeDtypeStruct((4 * PART + LANES, LANES), BF16)
    return pl.pallas_call(
        rows_body,
        in_specs=[SMEM] + [VMEM] * 4,
        out_specs=[VMEM] * 4,
        out_shape=[shape] * 4,
        compiler_params=SMALL_VMEM,
    )(place, mine, got, full, given)


def feature_body(j, h0, h1, h2, h3, slope, feats, out):
    total = None
    for k, part in enumerate((h0, h1, h2, h3)):
        floats = part[pl.ds(j * PART, LANES)].astype(F32)
        logistic = jax.nn.sigmoid(floats)
        slope[k] = logistic * (1.0 + floats * (1.0 - logistic))
        active = (floats * logistic).astype(BF16)
        basis = part[pl.ds(j * PART + LANES, RIN)]
        piece = jnp.dot(basis, active, preferred_element_type=F32)
        total = piece if total is None else total + piece
        out[:, k * LANES : (k + 1) * LANES] = part[pl.ds(j * PART + LANES + RIN, ROUT)]
    feats[...] = total


def features(here, j):
    return pl.pallas_call(
        lambda *refs: feature_body(j, *refs),
        in_specs=[VMEM] * 4,
        out_specs=[VMEM] * 3,
        out_shape=[
            jax.ShapeDtypeStruct((4, LANES, SEQ), F32),
            jax.ShapeDtypeStruct((RIN, SEQ), F32),
            jax.ShapeDtypeStruct((ROUT, 4 * LANES), BF16),
        ],
        compiler_params=SMALL_VMEM,
        name="features",
    )(*here)


def branch_body(place, c0, c1, c2, c3, out, w0, w1, low, high, w3, keep, send, feats, joined):
    z = place[2]
    feats[...] = jnp.dot(
        out[...], c0[...].reshape(4 * LANES, SEQ), preferred_element_type=F32
    )
    for m, ref in enumerate((c0, c1, c2, c3)):
        for block in range(4):
            joined[pl.ds((m * 4 + block) * LANES, LANES)] = ref[(block + 4 - z) % 4]
    for k, ref in ((0, w0), (1, w1), (3, w3)):
        part = jnp.dot(ref[...], joined[...], preferred_element_type=F32)
        keep[k] = part[:LANES]
        send[k] = part[LANES:]
    keep[2] = jnp.dot(low[...], joined[...], preferred_element_type=F32)
    send[2] = jnp.dot(high[...], joined[...], preferred_element_type=F32)


def branch(place, parts, basis, blocks):
    shape = jax.ShapeDtypeStruct((4, LANES, SEQ), F32)
    rows, depth = blocks[0].shape
    return pl.pallas_call(
        branch_body,
        in_specs=[SMEM] + [VMEM] * 10,
        out_specs=[VMEM] * 3,
        out_shape=[shape, shape, jax.ShapeDtypeStruct((ROUT, SEQ), F32)],
        scratch_shapes=[pltpu.VMEM((depth, SEQ), BF16)],
        compiler_params=pltpu.CompilerParams(vmem_limit_bytes=8 * 2**20),
        cost_estimate=pl.CostEstimate(
            flops=2 * SEQ * 4 * rows * depth,
            bytes_accessed=4 * rows * depth * 2,
            transcendentals=0,
        ),
    )(place, *parts, basis, *blocks)


def slope_of(hidden):
    floats = hidden.astype(F32)
    logistic = jax.nn.sigmoid(floats)
    return logistic * (1.0 + floats * (1.0 - logistic))


def activate(hidden):
    floats = hidden.astype(F32)
    return (floats * jax.nn.sigmoid(floats)).astype(BF16)


def first_fetch(block):
    return [shift(block, "z", 1), shift(block, "z", 3)]


def second_fetch(near):
    return [shift(near[0][:LANES], "z", 1), shift(near[1][LANES:], "z", 3)]


def shards(
    layer_inputs, weights, input_basis, output_basis, queries, top_cotangent, sequence_example
):
    x = lax.axis_index("x")
    core = lax.axis_index("c")
    z = lax.axis_index("z")
    y = lax.axis_index("y")
    is_top = x == 3
    tokens = layer_inputs.shape[1]
    width = layer_inputs.shape[2]
    flip = jnp.where(is_top & (core == 1), 0, 1)
    place = jnp.stack([core, y, z, flip]).astype(jnp.int32)

    upper = core == 1

    def over_width(part):
        own = lax.dynamic_slice_in_dim(part, 2 * core, 2, 0)
        half = own + shift(lax.dynamic_slice_in_dim(part, 2 - 2 * core, 2, 0), "c", 1)
        return half + sum(others(half, "y"))

    own_a, own_b, other_a, other_b = arrange(place, weights)
    own_w = (own_a, own_b)
    swapped = [shift(other_a, "c", 1), None]

    slots = [jnp.where(upper, own_w[0], swapped[0])]
    near = [first_fetch(slots[0])] + [None] * 3
    far = [None] * 4

    cotangent, other_b, inputs, _ = lax.optimization_barrier(
        (top_cotangent, other_b, layer_inputs, slots[0])
    )
    swapped[1] = shift(other_b, "c", 1)
    product = lax.dot_general(cotangent, weights[1], NT, preferred_element_type=F32)
    top_own = lax.dynamic_slice(top_cotangent, (0, (z * 4 + y) * width), (tokens, width))
    below_top = (top_own.astype(F32) + slope_of(layer_inputs[1]) * product).astype(BF16)
    given = shift(below_top[:, :LANES], "c", 1)

    mine, send = split(
        place, inputs, jnp.swapaxes(input_basis, 1, 2), jnp.swapaxes(output_basis, 1, 2)
    )
    outgoing = rows_of(place, mine, shift(send, "c", 1), below_top, given)

    near[0], outgoing = lax.optimization_barrier((near[0], outgoing))
    here = [outgoing[0]] + [shift(outgoing[k], "z", k) for k in (1, 2, 3)]
    near[0], here = lax.optimization_barrier((near[0], here))
    state = jnp.stack([part[4 * PART :] for part in here], 0)

    a0, a1, b0, b1 = lax.optimization_barrier((own_w[0], own_w[1], swapped[0], swapped[1]))
    slots.append(jnp.where(is_top, jnp.where(upper, b0, a0), jnp.where(upper, a1, b1)))
    slots.append(
        jnp.where(is_top, jnp.where(upper, b1, a1), jnp.where(upper, b0, a0))
    )
    slots.append(jnp.where(is_top, jnp.where(upper, a1, b1), jnp.where(upper, b1, a1)))

    slopes, in_part, out_basis = zip(*[features(here, j) for j in range(4)])
    in_part = jnp.stack(in_part, 0)
    examples = jnp.concatenate([sequence_example, sequence_example], 0)
    examples = lax.dynamic_slice_in_dim(examples, z, 4, 0)
    select = jnp.arange(EXAMPLES, dtype=jnp.int32)[:, None, None] == examples[None, :, None]
    select = select.astype(F32)
    in_part, select = lax.optimization_barrier((in_part, select))
    top_here = jnp.concatenate(
        [
            lax.dynamic_slice(
                top_cotangent,
                (z * SEQ, (z + k) % 4 * 1024 + y * 256 + core * LANES),
                (SEQ, LANES),
            )
            for k in range(4)
        ],
        1,
    )

    def advance(slot, parts):
        if slot > 0:
            near[slot], parts = lax.optimization_barrier((near[slot], parts))
        near[slot], slots[slot + 1] = lax.optimization_barrier((near[slot], slots[slot + 1]))
        far[slot] = second_fetch(near[slot])
        near[slot + 1] = first_fetch(slots[slot + 1])
        return parts

    out_part = [None] * 4
    for plane in (3, 2, 1, 0):
        for j in (3, 2, 1, 0):
            if plane == 3 and j == 3:
                out_part[j] = lax.dot_general(
                    out_basis[j], top_here, NT, preferred_element_type=F32
                )
                continue
            slot = 2 - j if plane == 3 else 3 - j
            parts = [state] + others(state, "y")
            if plane == 3:
                parts = advance(slot, parts)
            elif plane == 2 and slot == 1:
                near[3], parts = lax.optimization_barrier((near[3], parts))
                far[3] = second_fetch(near[3])
            blocks = [slots[slot], near[slot][0], far[slot][0], far[slot][1], near[slot][1]]
            keep, send, part = branch(place, parts, out_basis[j], blocks)
            if plane == 0 and j == 0:
                part = jnp.dot(out_basis[j], state.reshape(-1, SEQ), preferred_element_type=F32)
            out_part[j] = part if plane == 3 else jnp.where(x == plane, part, out_part[j])
            total = keep + shift(send, "c", 1)
            state = (state.astype(F32) + slopes[j] * total).astype(BF16)
            if plane == 3 and j == 1:
                in_part, state = lax.optimization_barrier((in_part, state))
                in_feats = over_width(in_part)
        if plane > 0:
            state = shift(state, "x", 1)

    out_feats = over_width(jnp.stack(out_part, 0))
    grads = jnp.einsum("jot,jit->joi", out_feats, in_feats, precision=HIGH)
    grads = grads.reshape(2, ROUT * RIN)
    rows = jnp.stack([grads] + others(grads, "z"), 1)
    scores = jnp.einsum("lsk,lqk->sq", rows, queries.astype(F32), precision=HIGH)
    scores = jnp.sum(jnp.where(select > 0, scores[None], 0.0), 1)
    scores = scores + shift(scores, "c", 1)
    return scores + sum(others(scores, "x"))


def solution(mesh):
    fine = Mesh(mesh.devices.reshape(4, 2, 4, 4), AXES)
    section = ("x", "c")
    tp = ("z", "y")
    placed = (
        P(section, None, tp),
        P(section, tp, None),
        P(section, tp, None),
        P(section, tp, None),
        P(section, tp, None),
        P(),
        P(),
    )
    return jax.shard_map(
        shards, mesh=fine, in_specs=placed, out_specs=P(None, tp), check_vma=False
    )
```

```python
import jax
import jax.numpy as jnp
from jax import lax
from jax.experimental import pallas as pl
from jax.experimental.pallas import tpu as pltpu
from jax.sharding import Mesh, PartitionSpec as P

AXES = ("x", "c", "z", "y")
SIZES = {"x": 4, "c": 2, "z": 4, "y": 4}
SEQ = 128
RIN = 64
ROUT = 32
PART = 128 + RIN + ROUT
LANES = 128
EXAMPLES = 2
F32 = jnp.float32
BF16 = jnp.bfloat16
HIGH = lax.Precision.HIGHEST
NT = (((1,), (1,)), ((), ()))


def shift(value, axis, by):
    size = SIZES[axis]
    return lax.ppermute(value, axis, [((i + by) % size, i) for i in range(size)])


def others(value, axis):
    return [shift(value, axis, by) for by in range(1, SIZES[axis])]


def arrange_body(place, source, own_a, own_b, other_a, other_b):
    core = place[0]
    y = place[1]
    for g, own, other in ((0, own_a, other_a), (1, own_b, other_b)):
        layer = (g + place[3]) % 2
        for m in range(4):
            for block in range(4):
                start = block * 1024 + ((y + m) % 4) * 256
                to = pl.ds((m * 4 + block) * LANES, LANES)
                mine = pl.multiple_of(start + core * LANES, LANES)
                theirs = pl.multiple_of(start + (1 - core) * LANES, LANES)
                own[:, to] = source[layer, :, pl.ds(mine, LANES)]
                other[:, to] = source[layer, :, pl.ds(theirs, LANES)]


def arrange(place, source):
    groups, rows, width = source.shape
    step = 64
    per = LANES // step
    own_map = lambda r, place: ((r // per + place[0]) % 2 * per + r % per, 0)
    other_map = lambda r, place: ((r // per + 1 - place[0]) % 2 * per + r % per, 0)
    half = (step, width // 2)
    shape = jax.ShapeDtypeStruct((rows, width // 2), source.dtype)
    return pl.pallas_call(
        arrange_body,
        grid_spec=pltpu.PrefetchScalarGridSpec(
            num_scalar_prefetch=1,
            grid=(rows // step,),
            in_specs=[pl.BlockSpec((groups, step, width), lambda r, place: (0, r, 0))],
            out_specs=[pl.BlockSpec(half, own_map)] * 2 + [pl.BlockSpec(half, other_map)] * 2,
        ),
        out_shape=[shape] * 4,
        compiler_params=pltpu.CompilerParams(vmem_limit_bytes=8 * 2**20),
    )(place, source)


SMALL_VMEM = pltpu.CompilerParams(vmem_limit_bytes=6 * 2**20)
VMEM = pl.BlockSpec(memory_space=pltpu.VMEM)
SMEM = pl.BlockSpec(memory_space=pltpu.SMEM)


def split_body(place, inputs, in_basis, out_basis, mine, send):
    core = place[0]
    tokens = inputs.shape[1]
    for target, half in ((mine, core), (send, 1 - core)):
        lanes = pl.ds(pl.multiple_of(half * LANES, LANES), LANES)
        for i in range(2):
            target[i, pl.ds(0, tokens)] = inputs[i, :, lanes]
            target[i, pl.ds(tokens, RIN)] = in_basis[i, :, lanes]
            target[i, pl.ds(tokens + RIN, ROUT)] = out_basis[i, :, lanes]


def split(place, inputs, in_basis, out_basis):
    shape = jax.ShapeDtypeStruct((2, inputs.shape[1] + RIN + ROUT, LANES), BF16)
    return pl.pallas_call(
        split_body,
        in_specs=[SMEM] + [VMEM] * 3,
        out_specs=[VMEM] * 2,
        out_shape=[shape] * 2,
        compiler_params=SMALL_VMEM,
    )(place, inputs, in_basis, out_basis)


def rows_body(place, mine, got, full, given, o0, o1, o2, o3):
    core = place[0]
    z = place[2]
    tokens = mine.shape[1] - RIN - ROUT
    for source, owner in ((mine, core), (got, 1 - core)):
        for i in range(2):
            layer = owner * 2 + i
            start = pl.multiple_of(layer * PART, 16)
            for k, target in enumerate((o0, o1, o2, o3)):
                at = pl.multiple_of((z + 4 - k) % 4 * SEQ, SEQ)
                target[pl.ds(start, LANES)] = source[i, pl.ds(at, SEQ)].T
                target[pl.ds(start + LANES, RIN + ROUT)] = source[i, pl.ds(tokens, RIN + ROUT)]
    for k, target in enumerate((o0, o1, o2, o3)):
        at = pl.ds(pl.multiple_of((z + 4 - k) % 4 * SEQ, SEQ), SEQ)
        own = full[at, LANES:].astype(F32)
        other = given[at].astype(F32)
        target[pl.ds(4 * PART, LANES)] = jnp.where(core == 1, own, other).T.astype(BF16)


def rows_of(place, mine, got, full, given):
    shape = jax.ShapeDtypeStruct((4 * PART + LANES, LANES), BF16)
    return pl.pallas_call(
        rows_body,
        in_specs=[SMEM] + [VMEM] * 4,
        out_specs=[VMEM] * 4,
        out_shape=[shape] * 4,
        compiler_params=SMALL_VMEM,
    )(place, mine, got, full, given)


def feature_body(j, h0, h1, h2, h3, slope, feats, out):
    total = None
    for k, part in enumerate((h0, h1, h2, h3)):
        floats = part[pl.ds(j * PART, LANES)].astype(F32)
        logistic = jax.nn.sigmoid(floats)
        slope[k] = logistic * (1.0 + floats * (1.0 - logistic))
        active = (floats * logistic).astype(BF16)
        basis = part[pl.ds(j * PART + LANES, RIN)]
        piece = jnp.dot(basis, active, preferred_element_type=F32)
        total = piece if total is None else total + piece
        out[:, k * LANES : (k + 1) * LANES] = part[pl.ds(j * PART + LANES + RIN, ROUT)]
    feats[...] = total


def features(here, j):
    return pl.pallas_call(
        lambda *refs: feature_body(j, *refs),
        in_specs=[VMEM] * 4,
        out_specs=[VMEM] * 3,
        out_shape=[
            jax.ShapeDtypeStruct((4, LANES, SEQ), F32),
            jax.ShapeDtypeStruct((RIN, SEQ), F32),
            jax.ShapeDtypeStruct((ROUT, 4 * LANES), BF16),
        ],
        compiler_params=SMALL_VMEM,
        name="features",
    )(*here)


def branch_body(place, c0, c1, c2, c3, out, w0, w1, low, high, w3, keep, send, feats, joined):
    z = place[2]
    feats[...] = jnp.dot(
        out[...], c0[...].reshape(4 * LANES, SEQ), preferred_element_type=F32
    )
    for m, ref in enumerate((c0, c1, c2, c3)):
        for block in range(4):
            joined[pl.ds((m * 4 + block) * LANES, LANES)] = ref[(block + 4 - z) % 4]
    for k, ref in ((0, w0), (1, w1), (3, w3)):
        part = jnp.dot(ref[...], joined[...], preferred_element_type=F32)
        keep[k] = part[:LANES]
        send[k] = part[LANES:]
    keep[2] = jnp.dot(low[...], joined[...], preferred_element_type=F32)
    send[2] = jnp.dot(high[...], joined[...], preferred_element_type=F32)


def branch(place, parts, basis, blocks):
    shape = jax.ShapeDtypeStruct((4, LANES, SEQ), F32)
    rows, depth = blocks[0].shape
    return pl.pallas_call(
        branch_body,
        in_specs=[SMEM] + [VMEM] * 10,
        out_specs=[VMEM] * 3,
        out_shape=[shape, shape, jax.ShapeDtypeStruct((ROUT, SEQ), F32)],
        scratch_shapes=[pltpu.VMEM((depth, SEQ), BF16)],
        compiler_params=pltpu.CompilerParams(vmem_limit_bytes=8 * 2**20),
        cost_estimate=pl.CostEstimate(
            flops=2 * SEQ * 4 * rows * depth,
            bytes_accessed=4 * rows * depth * 2,
            transcendentals=0,
        ),
    )(place, *parts, basis, *blocks)


def slope_of(hidden):
    floats = hidden.astype(F32)
    logistic = jax.nn.sigmoid(floats)
    return logistic * (1.0 + floats * (1.0 - logistic))


def activate(hidden):
    floats = hidden.astype(F32)
    return (floats * jax.nn.sigmoid(floats)).astype(BF16)


def first_fetch(block):
    return [shift(block, "z", 1), shift(block, "z", 3)]


def second_fetch(near):
    return [shift(near[0][:LANES], "z", 1), shift(near[1][LANES:], "z", 3)]


def shards(
    layer_inputs, weights, input_basis, output_basis, queries, top_cotangent, sequence_example
):
    x = lax.axis_index("x")
    core = lax.axis_index("c")
    z = lax.axis_index("z")
    y = lax.axis_index("y")
    is_top = x == 3
    tokens = layer_inputs.shape[1]
    width = layer_inputs.shape[2]
    flip = jnp.where(is_top & (core == 1), 0, 1)
    place = jnp.stack([core, y, z, flip]).astype(jnp.int32)

    upper = core == 1

    def over_chip(part):
        own = lax.dynamic_slice_in_dim(part, 2 * core, 2, 0)
        return own + shift(lax.dynamic_slice_in_dim(part, 2 - 2 * core, 2, 0), "c", 1)

    def over_width(part):
        half = over_chip(part)
        return half + sum(others(half, "y"))

    own_a, own_b, other_a, other_b = arrange(place, weights)
    own_w = (own_a, own_b)
    swapped = [shift(other_a, "c", 1), None]

    slots = [jnp.where(upper, own_w[0], swapped[0])]
    near = [first_fetch(slots[0])] + [None] * 3
    far = [None] * 4

    cotangent, other_b, inputs, _ = lax.optimization_barrier(
        (top_cotangent, other_b, layer_inputs, slots[0])
    )
    swapped[1] = shift(other_b, "c", 1)
    product = lax.dot_general(cotangent, weights[1], NT, preferred_element_type=F32)
    top_own = lax.dynamic_slice(top_cotangent, (0, (z * 4 + y) * width), (tokens, width))
    below_top = (top_own.astype(F32) + slope_of(layer_inputs[1]) * product).astype(BF16)
    given = shift(below_top[:, :LANES], "c", 1)

    mine, send = split(
        place, inputs, jnp.swapaxes(input_basis, 1, 2), jnp.swapaxes(output_basis, 1, 2)
    )
    outgoing = rows_of(place, mine, shift(send, "c", 1), below_top, given)

    near[0], outgoing = lax.optimization_barrier((near[0], outgoing))
    here = [outgoing[0]] + [shift(outgoing[k], "z", k) for k in (1, 2, 3)]
    near[0], here = lax.optimization_barrier((near[0], here))
    state = jnp.stack([part[4 * PART :] for part in here], 0)

    a0, a1, b0, b1 = lax.optimization_barrier((own_w[0], own_w[1], swapped[0], swapped[1]))
    slots.append(jnp.where(is_top, jnp.where(upper, b0, a0), jnp.where(upper, a1, b1)))
    slots.append(
        jnp.where(is_top, jnp.where(upper, b1, a1), jnp.where(upper, b0, a0))
    )
    slots.append(jnp.where(is_top, jnp.where(upper, a1, b1), jnp.where(upper, b1, a1)))

    slopes, in_part, out_basis = zip(*[features(here, j) for j in range(4)])
    in_part = jnp.stack(in_part, 0)
    select = jnp.arange(EXAMPLES, dtype=jnp.int32)[:, None, None] == sequence_example[None, :, None]
    select = select.astype(F32)
    in_part, select = lax.optimization_barrier((in_part, select))
    top_here = jnp.concatenate(
        [
            lax.dynamic_slice(
                top_cotangent,
                (z * SEQ, (z + k) % 4 * 1024 + y * 256 + core * LANES),
                (SEQ, LANES),
            )
            for k in range(4)
        ],
        1,
    )

    def advance(slot, parts):
        if slot > 0:
            near[slot], parts = lax.optimization_barrier((near[slot], parts))
        near[slot], slots[slot + 1] = lax.optimization_barrier((near[slot], slots[slot + 1]))
        far[slot] = second_fetch(near[slot])
        near[slot + 1] = first_fetch(slots[slot + 1])
        return parts

    out_part = [None] * 4
    for plane in (3, 2, 1, 0):
        for j in (3, 2, 1, 0):
            if plane == 3 and j == 3:
                out_part[j] = lax.dot_general(
                    out_basis[j], top_here, NT, preferred_element_type=F32
                )
                continue
            slot = 2 - j if plane == 3 else 3 - j
            parts = [state] + others(state, "y")
            if plane == 3:
                parts = advance(slot, parts)
            elif plane == 2 and slot == 1:
                near[3], parts = lax.optimization_barrier((near[3], parts))
                far[3] = second_fetch(near[3])
            elif plane == 2 and slot == 2:
                far[3], parts = lax.optimization_barrier((far[3], parts))
            blocks = [slots[slot], near[slot][0], far[slot][0], far[slot][1], near[slot][1]]
            keep, send, part = branch(place, parts, out_basis[j], blocks)
            if plane == 0 and j == 0:
                part = jnp.dot(out_basis[j], state.reshape(-1, SEQ), preferred_element_type=F32)
            out_part[j] = part if plane == 3 else jnp.where(x == plane, part, out_part[j])
            total = keep + shift(send, "c", 1)
            state = (state.astype(F32) + slopes[j] * total).astype(BF16)
            if plane == 3 and j == 1:
                in_part, state = lax.optimization_barrier((in_part, state))
                in_feats = over_width(in_part)
        if plane > 0:
            state = shift(state, "x", 1)

    out_feats = over_chip(jnp.stack(out_part, 0))
    grads = jnp.einsum("jot,jit->joi", out_feats, in_feats, precision=HIGH)
    grads = jnp.broadcast_to(grads.reshape(1, 2, ROUT * RIN), (16, 2, ROUT * RIN))
    grads = lax.all_to_all(grads, ("z", "y"), 0, 0)
    rows = jnp.sum(grads.reshape(4, 4, 2, ROUT * RIN), 1)
    scores = jnp.einsum("slk,lqk->sq", rows, queries.astype(F32), precision=HIGH)
    scores = jnp.sum(jnp.where(select > 0, scores[None], 0.0), 1)
    scores = scores + shift(scores, "c", 1)
    return scores + sum(others(scores, "x"))


def solution(mesh):
    fine = Mesh(mesh.devices.reshape(4, 2, 4, 4), AXES)
    section = ("x", "c")
    tp = ("z", "y")
    placed = (
        P(section, None, tp),
        P(section, tp, None),
        P(section, tp, None),
        P(section, tp, None),
        P(section, tp, None),
        P(),
        P(),
    )
    return jax.shard_map(
        shards, mesh=fine, in_specs=placed, out_specs=P(None, tp), check_vma=False
    )
```

```python
import jax
import jax.numpy as jnp
from jax import lax
from jax.experimental import pallas as pl
from jax.experimental.pallas import tpu as pltpu
from jax.sharding import Mesh, PartitionSpec as P

AXES = ("x", "c", "z", "y")
SIZES = {"x": 4, "c": 2, "z": 4, "y": 4}
SEQ = 128
RIN = 64
ROUT = 32
PART = 128 + RIN + ROUT
LANES = 128
EXAMPLES = 2
F32 = jnp.float32
BF16 = jnp.bfloat16
HIGH = lax.Precision.HIGHEST
NT = (((1,), (1,)), ((), ()))


def shift(value, axis, by):
    size = SIZES[axis]
    return lax.ppermute(value, axis, [((i + by) % size, i) for i in range(size)])


def others(value, axis):
    return [shift(value, axis, by) for by in range(1, SIZES[axis])]


def arrange_body(place, source, own_a, own_b, other_a, other_b):
    core = place[0]
    y = place[1]
    for g, own, other in ((0, own_a, other_a), (1, own_b, other_b)):
        layer = (g + place[3]) % 2
        for m in range(4):
            for block in range(4):
                start = block * 1024 + ((y + m) % 4) * 256
                to = pl.ds((m * 4 + block) * LANES, LANES)
                mine = pl.multiple_of(start + core * LANES, LANES)
                theirs = pl.multiple_of(start + (1 - core) * LANES, LANES)
                own[:, to] = source[layer, :, pl.ds(mine, LANES)]
                other[:, to] = source[layer, :, pl.ds(theirs, LANES)]


def arrange(place, source):
    groups, rows, width = source.shape
    step = 64
    per = LANES // step
    own_map = lambda r, place: ((r // per + place[0]) % 2 * per + r % per, 0)
    other_map = lambda r, place: ((r // per + 1 - place[0]) % 2 * per + r % per, 0)
    half = (step, width // 2)
    shape = jax.ShapeDtypeStruct((rows, width // 2), source.dtype)
    return pl.pallas_call(
        arrange_body,
        grid_spec=pltpu.PrefetchScalarGridSpec(
            num_scalar_prefetch=1,
            grid=(rows // step,),
            in_specs=[pl.BlockSpec((groups, step, width), lambda r, place: (0, r, 0))],
            out_specs=[pl.BlockSpec(half, own_map)] * 2 + [pl.BlockSpec(half, other_map)] * 2,
        ),
        out_shape=[shape] * 4,
        compiler_params=pltpu.CompilerParams(vmem_limit_bytes=8 * 2**20),
    )(place, source)


SMALL_VMEM = pltpu.CompilerParams(vmem_limit_bytes=6 * 2**20)
VMEM = pl.BlockSpec(memory_space=pltpu.VMEM)
SMEM = pl.BlockSpec(memory_space=pltpu.SMEM)


def split_body(place, inputs, in_basis, out_basis, mine, send):
    core = place[0]
    tokens = inputs.shape[1]
    for target, half in ((mine, core), (send, 1 - core)):
        lanes = pl.ds(pl.multiple_of(half * LANES, LANES), LANES)
        for i in range(2):
            target[i, pl.ds(0, tokens)] = inputs[i, :, lanes]
            target[i, pl.ds(tokens, RIN)] = in_basis[i, :, lanes]
            target[i, pl.ds(tokens + RIN, ROUT)] = out_basis[i, :, lanes]


def split(place, inputs, in_basis, out_basis):
    shape = jax.ShapeDtypeStruct((2, inputs.shape[1] + RIN + ROUT, LANES), BF16)
    return pl.pallas_call(
        split_body,
        in_specs=[SMEM] + [VMEM] * 3,
        out_specs=[VMEM] * 2,
        out_shape=[shape] * 2,
        compiler_params=SMALL_VMEM,
    )(place, inputs, in_basis, out_basis)


def rows_body(place, mine, got, full, given, o0, o1, o2, o3):
    core = place[0]
    z = place[2]
    tokens = mine.shape[1] - RIN - ROUT
    for source, owner in ((mine, core), (got, 1 - core)):
        for i in range(2):
            layer = owner * 2 + i
            start = pl.multiple_of(layer * PART, 16)
            for k, target in enumerate((o0, o1, o2, o3)):
                at = pl.multiple_of((z + 4 - k) % 4 * SEQ, SEQ)
                target[pl.ds(start, LANES)] = source[i, pl.ds(at, SEQ)].T
                target[pl.ds(start + LANES, RIN + ROUT)] = source[i, pl.ds(tokens, RIN + ROUT)]
    for k, target in enumerate((o0, o1, o2, o3)):
        at = pl.ds(pl.multiple_of((z + 4 - k) % 4 * SEQ, SEQ), SEQ)
        own = full[at, LANES:].astype(F32)
        other = given[at].astype(F32)
        target[pl.ds(4 * PART, LANES)] = jnp.where(core == 1, own, other).T.astype(BF16)


def rows_of(place, mine, got, full, given):
    shape = jax.ShapeDtypeStruct((4 * PART + LANES, LANES), BF16)
    return pl.pallas_call(
        rows_body,
        in_specs=[SMEM] + [VMEM] * 4,
        out_specs=[VMEM] * 4,
        out_shape=[shape] * 4,
        compiler_params=SMALL_VMEM,
    )(place, mine, got, full, given)


def feature_body(j, h0, h1, h2, h3, slope, feats, out):
    total = None
    for k, part in enumerate((h0, h1, h2, h3)):
        floats = part[pl.ds(j * PART, LANES)].astype(F32)
        logistic = jax.nn.sigmoid(floats)
        slope[k] = logistic * (1.0 + floats * (1.0 - logistic))
        active = (floats * logistic).astype(BF16)
        basis = part[pl.ds(j * PART + LANES, RIN)]
        piece = jnp.dot(basis, active, preferred_element_type=F32)
        total = piece if total is None else total + piece
        out[:, k * LANES : (k + 1) * LANES] = part[pl.ds(j * PART + LANES + RIN, ROUT)]
    feats[...] = total


def features(here, j):
    return pl.pallas_call(
        lambda *refs: feature_body(j, *refs),
        in_specs=[VMEM] * 4,
        out_specs=[VMEM] * 3,
        out_shape=[
            jax.ShapeDtypeStruct((4, LANES, SEQ), F32),
            jax.ShapeDtypeStruct((RIN, SEQ), F32),
            jax.ShapeDtypeStruct((ROUT, 4 * LANES), BF16),
        ],
        compiler_params=SMALL_VMEM,
        name="features",
    )(*here)


def branch_body(place, c0, c1, c2, c3, out, w0, w1, low, high, w3, keep, send, feats, joined):
    z = place[2]
    feats[...] = jnp.dot(
        out[...], c0[...].reshape(4 * LANES, SEQ), preferred_element_type=F32
    )
    for m, ref in enumerate((c0, c1, c2, c3)):
        for block in range(4):
            joined[pl.ds((m * 4 + block) * LANES, LANES)] = ref[(block + 4 - z) % 4]
    for k, ref in ((0, w0), (1, w1), (3, w3)):
        part = jnp.dot(ref[...], joined[...], preferred_element_type=F32)
        keep[k] = part[:LANES]
        send[k] = part[LANES:]
    keep[2] = jnp.dot(low[...], joined[...], preferred_element_type=F32)
    send[2] = jnp.dot(high[...], joined[...], preferred_element_type=F32)


def late_body(*refs):
    sources, outs, joined = refs[6:11], refs[11:14], refs[14]
    held, sems = refs[15:20], refs[20]
    copies = [
        pltpu.make_async_copy(source, target, sems.at[n])
        for n, (source, target) in enumerate(zip(sources, held))
    ]
    for copy in copies:
        copy.start()
    for copy in copies:
        copy.wait()
    branch_body(*refs[:6], *held, *outs, joined)


def branch(place, parts, basis, blocks, late):
    shape = jax.ShapeDtypeStruct((4, LANES, SEQ), F32)
    rows, depth = blocks[0].shape
    own = [pltpu.VMEM(block.shape, BF16) for block in blocks] + [pltpu.SemaphoreType.DMA((5,))]
    own = own if late else []
    return pl.pallas_call(
        late_body if late else branch_body,
        in_specs=[SMEM] + [VMEM] * 5 + [pl.BlockSpec(memory_space=pl.ANY) if late else VMEM] * 5,
        out_specs=[VMEM] * 3,
        out_shape=[shape, shape, jax.ShapeDtypeStruct((ROUT, SEQ), F32)],
        scratch_shapes=[pltpu.VMEM((depth, SEQ), BF16)] + own,
        compiler_params=pltpu.CompilerParams(vmem_limit_bytes=12 * 2**20 if late else 8 * 2**20),
        cost_estimate=pl.CostEstimate(
            flops=2 * SEQ * 4 * rows * depth,
            bytes_accessed=4 * rows * depth * 2,
            transcendentals=0,
        ),
    )(place, *parts, basis, *blocks)


def slope_of(hidden):
    floats = hidden.astype(F32)
    logistic = jax.nn.sigmoid(floats)
    return logistic * (1.0 + floats * (1.0 - logistic))


def activate(hidden):
    floats = hidden.astype(F32)
    return (floats * jax.nn.sigmoid(floats)).astype(BF16)


def first_fetch(block):
    return [shift(block, "z", 1), shift(block, "z", 3)]


def second_fetch(near):
    return [shift(near[0][:LANES], "z", 1), shift(near[1][LANES:], "z", 3)]


def shards(
    layer_inputs, weights, input_basis, output_basis, queries, top_cotangent, sequence_example
):
    x = lax.axis_index("x")
    core = lax.axis_index("c")
    z = lax.axis_index("z")
    y = lax.axis_index("y")
    is_top = x == 3
    tokens = layer_inputs.shape[1]
    width = layer_inputs.shape[2]
    flip = jnp.where(is_top & (core == 1), 0, 1)
    place = jnp.stack([core, y, z, flip]).astype(jnp.int32)

    upper = core == 1

    def over_chip(part):
        own = lax.dynamic_slice_in_dim(part, 2 * core, 2, 0)
        return own + shift(lax.dynamic_slice_in_dim(part, 2 - 2 * core, 2, 0), "c", 1)

    def over_width(part):
        half = over_chip(part)
        return half + sum(others(half, "y"))

    own_a, own_b, other_a, other_b = arrange(place, weights)
    own_w = (own_a, own_b)
    swapped = [shift(other_a, "c", 1), None]

    slots = [jnp.where(upper, own_w[0], swapped[0])]
    near = [first_fetch(slots[0])] + [None] * 3
    far = [None] * 4

    cotangent, other_b, inputs, _ = lax.optimization_barrier(
        (top_cotangent, other_b, layer_inputs, slots[0])
    )
    swapped[1] = shift(other_b, "c", 1)
    product = lax.dot_general(cotangent, weights[1], NT, preferred_element_type=F32)
    top_own = lax.dynamic_slice(top_cotangent, (0, (z * 4 + y) * width), (tokens, width))
    below_top = (top_own.astype(F32) + slope_of(layer_inputs[1]) * product).astype(BF16)
    given = shift(below_top[:, :LANES], "c", 1)

    mine, send = split(
        place, inputs, jnp.swapaxes(input_basis, 1, 2), jnp.swapaxes(output_basis, 1, 2)
    )
    outgoing = rows_of(place, mine, shift(send, "c", 1), below_top, given)

    near[0], outgoing = lax.optimization_barrier((near[0], outgoing))
    here = [outgoing[0]] + [shift(outgoing[k], "z", k) for k in (1, 2, 3)]
    near[0], here = lax.optimization_barrier((near[0], here))
    state = jnp.stack([part[4 * PART :] for part in here], 0)

    a0, a1, b0, b1 = lax.optimization_barrier((own_w[0], own_w[1], swapped[0], swapped[1]))
    slots.append(jnp.where(is_top, jnp.where(upper, b0, a0), jnp.where(upper, a1, b1)))
    slots.append(
        jnp.where(is_top, jnp.where(upper, b1, a1), jnp.where(upper, b0, a0))
    )
    slots.append(jnp.where(is_top, jnp.where(upper, a1, b1), jnp.where(upper, b1, a1)))

    slopes, in_part, out_basis = zip(*[features(here, j) for j in range(4)])
    in_part = jnp.stack(in_part, 0)
    select = jnp.arange(EXAMPLES, dtype=jnp.int32)[:, None, None] == sequence_example[None, :, None]
    select = select.astype(F32)
    in_part, select = lax.optimization_barrier((in_part, select))
    top_here = jnp.concatenate(
        [
            lax.dynamic_slice(
                top_cotangent,
                (z * SEQ, (z + k) % 4 * 1024 + y * 256 + core * LANES),
                (SEQ, LANES),
            )
            for k in range(4)
        ],
        1,
    )

    def advance(slot, parts):
        if slot > 0:
            near[slot], parts = lax.optimization_barrier((near[slot], parts))
        near[slot], slots[slot + 1] = lax.optimization_barrier((near[slot], slots[slot + 1]))
        far[slot] = second_fetch(near[slot])
        near[slot + 1] = first_fetch(slots[slot + 1])
        return parts

    out_part = [None] * 4
    for plane in (3, 2, 1, 0):
        for j in (3, 2, 1, 0):
            if plane == 3 and j == 3:
                out_part[j] = lax.dot_general(
                    out_basis[j], top_here, NT, preferred_element_type=F32
                )
                continue
            slot = 2 - j if plane == 3 else 3 - j
            parts = [state] + others(state, "y")
            if plane == 3:
                parts = advance(slot, parts)
            elif plane == 2 and slot == 1:
                near[3], parts = lax.optimization_barrier((near[3], parts))
                far[3] = second_fetch(near[3])
            elif plane == 2 and slot == 2:
                far[3], parts = lax.optimization_barrier((far[3], parts))
            blocks = [slots[slot], near[slot][0], far[slot][0], far[slot][1], near[slot][1]]
            keep, send, part = branch(place, parts, out_basis[j], blocks, plane == 0 and j < 3)
            if plane == 0 and j == 0:
                part = jnp.dot(out_basis[j], state.reshape(-1, SEQ), preferred_element_type=F32)
            out_part[j] = part if plane == 3 else jnp.where(x == plane, part, out_part[j])
            total = keep + shift(send, "c", 1)
            state = (state.astype(F32) + slopes[j] * total).astype(BF16)
            if plane == 3 and j == 1:
                in_part, state = lax.optimization_barrier((in_part, state))
                in_feats = over_width(in_part)
        if plane > 0:
            state = shift(state, "x", 1)

    out_feats = over_chip(jnp.stack(out_part, 0))
    grads = jnp.einsum("jot,jit->joi", out_feats, in_feats, precision=HIGH)
    grads = jnp.broadcast_to(grads.reshape(1, 2, ROUT * RIN), (16, 2, ROUT * RIN))
    grads = lax.all_to_all(grads, ("z", "y"), 0, 0)
    rows = jnp.sum(grads.reshape(4, 4, 2, ROUT * RIN), 1)
    scores = jnp.einsum("slk,lqk->sq", rows, queries.astype(F32), precision=HIGH)
    scores = jnp.sum(jnp.where(select > 0, scores[None], 0.0), 1)
    scores = scores + shift(scores, "c", 1)
    return scores + sum(others(scores, "x"))


def solution(mesh):
    fine = Mesh(mesh.devices.reshape(4, 2, 4, 4), AXES)
    section = ("x", "c")
    tp = ("z", "y")
    placed = (
        P(section, None, tp),
        P(section, tp, None),
        P(section, tp, None),
        P(section, tp, None),
        P(section, tp, None),
        P(),
        P(),
    )
    return jax.shard_map(
        shards, mesh=fine, in_specs=placed, out_specs=P(None, tp), check_vma=False
    )
```
